1024 devices in a mesh: dp: 64 (over z, core), seq: 8 (over y_lo, x), mp: 2 (over y_hi).
Axes of the slice: x: 4, y: 4 (y_hi: 2, y_lo: 2; y = y_hi * 2 + y_lo), z: 32, core: 2. Of those that a mesh axis runs over, the one named last changes fastest.
Arguments:
- queries: bfloat16 [64, 1024, 768], P('dp', 'seq', 'mp'), may hold values from -60 to 60
- keys: bfloat16 [64, 1024, 768], P('dp', 'seq', 'mp'), may hold values from -8 to 8
- values: bfloat16 [64, 1024, 768], P('dp', 'seq', 'mp'), may hold values from -6 to 6
- proj_weight: bfloat16 [2, 384, 1536], P('mp', 'dp'), may hold values from -0.5 to 0.5
- gate_table: float32 [4, 1536], replicated, may hold values from -6 to 6
- timestep: int32 [64], P('dp'), may hold values from 0 to 3
- span_index: int32 [64], P('dp'), may hold values from 0 to 7
- cotangent: bfloat16 [64, 1024, 1536], P('dp', 'seq'), may hold values from -0.0625 to 0.0625
Outputs:
- output: bfloat16 [64, 1024, 1536], P('dp', ('seq', 'mp'))
- weight_grad: float32 [2, 4608, 128], P('mp', ('dp', 'seq'))
The draws below stay inside these ranges and needn't reach their ends.
All inputs are finite; a program needn't handle non-finite values.
Results may differ from the reference program's by a relative error of at most 0.015.
Values may be sent and summed in bfloat16 or wider, within the bound.
No kernel may reach another device: no remote copies, remote signals or barrier semaphores. Data moves between devices by JAX's collectives and lax.ppermute only.
A program may use at most 32 MiB of HBM per device.

```python
import jax
import jax.numpy as jnp
from jax import lax

D = 1536
HEAD = 128
HEADS = 6
STEPS = 4
TOK_DEV = 128
HD = 768
HDM = 384
ROLLOUTS = 64
SPANS = 8
SEQLEN = 1024
GRAD_ROWS = 4608
N_MP = 2


def paired_draw(key):
    base = jax.random.fold_in(key, 11)
    first, second = jax.random.split(base)
    shape = (ROLLOUTS, SEQLEN, HD)
    key_field = 1.5 * jax.random.truncated_normal(first, -4.0, 4.0, shape, jnp.float32)
    query_field = 1.5 * jax.random.truncated_normal(second, -4.0, 4.0, shape, jnp.float32)
    return (query_field, key_field)


def draw_queries(key, part):
    return paired_draw(key)[0].astype(jnp.bfloat16)


def draw_keys(key, part):
    return paired_draw(key)[1].astype(jnp.bfloat16)


def with_ends(array, stream_key, low, top_value):
    longest = array.shape.index(max(array.shape))
    spots = []
    for shift in (0, 1):
        where = [jax.random.randint(jax.random.fold_in(stream_key, axis), (), 0, length) for axis, length in enumerate(array.shape)]
        where[longest] = (where[longest] + shift) % array.shape[longest]
        spots.append(tuple(where))
    return array.at[spots[0]].set(low).at[spots[1]].set(top_value)


def block_levels(stream_key, shape, shards, least, largest):
    gain = 1.0
    for position, blocks in shards:
        draws = jax.random.uniform(jax.random.fold_in(jax.random.fold_in(stream_key, 6), position), (blocks,), jnp.float32, least / len(shards), largest / len(shards))
        gain = gain * jnp.repeat(jnp.exp(draws), shape[position] // blocks).reshape((-1,) + (1,) * (len(shape) - 1 - position))
    return gain


def gaussian(key, shape, spread, bound, shards=(), kind=jnp.bfloat16):
    values = spread * jax.random.normal(key, shape, jnp.float32)
    if shards:
        values = values * block_levels(key, shape, shards, -0.22, 0.18)
    return jnp.clip(values, -bound, bound).astype(kind)


def setup_inputs(seed: int = 0) -> dict:
    arg_keys = jax.random.split(jax.random.key(seed), 9)
    return {
        "queries": draw_queries(jax.random.fold_in(arg_keys[8], 71), 0),
        "keys": draw_keys(jax.random.fold_in(arg_keys[8], 71), 0),
        "values": gaussian(arg_keys[2], (ROLLOUTS, SEQLEN, HD), 1.0, 6.0, ((0, 64), (1, 8), (2, 2))),
        "proj_weight": gaussian(arg_keys[3], (N_MP, HDM, D), HEAD ** -0.5, 0.5, ((0, 2), (1, 64))),
        "gate_table": gaussian(arg_keys[4], (STEPS, D), 1.0, 6.0, (), jnp.float32),
        "timestep": with_ends(jax.random.randint(arg_keys[5], (ROLLOUTS,), 0, STEPS), jax.random.fold_in(arg_keys[5], 1), 0, STEPS - 1).astype(jnp.int32),
        "span_index": with_ends(jax.random.randint(arg_keys[6], (ROLLOUTS,), 0, SPANS), jax.random.fold_in(arg_keys[6], 1), 0, SPANS - 1).astype(jnp.int32),
        "cotangent": gaussian(arg_keys[7], (ROLLOUTS, SEQLEN, D), 0.01, 0.0625, ((0, 64), (1, 8))),
    }


def reference(queries, keys, values, proj_weight, gate_table, timestep, span_index, cotangent):
    inv_root = HEAD ** -0.5
    positions = jnp.arange(SEQLEN, dtype=jnp.int32)
    span_of = positions // TOK_DEV
    weight_full = proj_weight.reshape(HD, D)

    def one_rollout(grad_sum, items):
        query_rows, key_rows, value_rows, step_id, last_span, cot_rows = items
        query_heads = query_rows.reshape(SEQLEN, HEADS, HEAD).astype(jnp.float32)
        key_heads = key_rows.reshape(SEQLEN, HEADS, HEAD).astype(jnp.float32)
        value_heads = value_rows.reshape(SEQLEN, HEADS, HEAD).astype(jnp.float32)
        scores = jnp.einsum('qhd,khd->hqk', query_heads, key_heads) * inv_root
        limit = jnp.minimum(span_of, last_span)
        visible = span_of[None, :] <= limit[:, None]
        scores = jnp.where(visible[None], scores, -jnp.inf)
        row_top = jnp.max(scores, axis=2, keepdims=True)
        weights = jnp.exp(scores - row_top)
        probs = (weights / jnp.sum(weights, axis=2, keepdims=True)).astype(jnp.bfloat16)
        attended = jnp.einsum('hqk,khd->qhd', probs.astype(jnp.float32), value_heads)
        attended = attended.reshape(SEQLEN, HD).astype(jnp.bfloat16)
        mixed = jnp.dot(attended, weight_full, preferred_element_type=jnp.float32)
        gate = gate_table[step_id]
        output = (gate[None, :] * mixed).astype(jnp.bfloat16)
        scaled = (gate[None, :] * cot_rows.astype(jnp.float32)).astype(jnp.bfloat16)
        grad_sum = grad_sum + jnp.dot(attended.T, scaled, preferred_element_type=jnp.float32)
        return grad_sum, output

    start_grad = jnp.zeros((HD, D), jnp.float32)
    grad_sum, output = lax.scan(one_rollout, start_grad, (queries, keys, values, timestep, span_index, cotangent))
    weight_grad = grad_sum.reshape(N_MP, GRAD_ROWS, 128)
    return output, weight_grad
```

```python
import jax
import jax.numpy as jnp
from jax import lax
from jax.experimental import pallas as pl
from jax.experimental.pallas import tpu as pltpu
from jax.sharding import Mesh, PartitionSpec as P

HEAD = 128
TOK = 128
SPANS = 8
ZS = 32
WIDTH = 1536
HDM = 384
CHUNK = 1152
TAIL = WIDTH - CHUNK
SEQ = ("yl", "x")
F32 = jnp.float32
BF16 = jnp.bfloat16
VM = pl.BlockSpec(memory_space=pltpu.VMEM)
SM = pl.BlockSpec(memory_space=pltpu.SMEM)


def nt_dot(a, b):
    return lax.dot_general(a, b, (((1,), (1,)), ((), ())), preferred_element_type=F32)


def spread_kernel(w_ref, out_ref):
    w = w_ref[0].astype(F32)
    tail = w[:, CHUNK:]
    rows = [
        jnp.concatenate([tail[3 * r + s : 3 * r + s + 1] for s in range(3)], axis=1)
        for r in range(2)
    ]
    block = jnp.concatenate([w[:, :CHUNK]] + rows, axis=0).astype(BF16)
    for z in range(ZS):
        out_ref[z] = block


def attend_kernel(ts_ref, si_ref, q_ref, kv_ref, cot_ref, table_ref, keep_ref, send_ref, att_ref, gate_ref):
    place = lax.axis_index("yl") * 4 + lax.axis_index("x")
    core = lax.axis_index("c")
    limit = jnp.minimum(place, si_ref[0])
    inv_root = HEAD ** (-0.5)
    spans = lax.broadcasted_iota(jnp.int32, (1, SPANS * TOK), 1) // TOK
    visible = spans <= limit
    outs = []
    for h in range(HDM // HEAD):
        cols = slice(h * HEAD, (h + 1) * HEAD)
        keys = jnp.concatenate([kv_ref[j, :TOK, cols] for j in range(SPANS)], axis=0)
        values = jnp.concatenate([kv_ref[j, TOK:, cols] for j in range(SPANS)], axis=0)
        scores = nt_dot(q_ref[0, :, cols], keys) * inv_root
        scores = jnp.where(visible, scores, -jnp.inf)
        weights = jnp.exp(scores - jnp.max(scores, axis=1, keepdims=True))
        probs = (weights / jnp.sum(weights, axis=1, keepdims=True)).astype(BF16)
        outs.append(jnp.dot(probs, values, preferred_element_type=F32).astype(BF16))
    attended = jnp.concatenate(outs, axis=1)
    att_ref[...] = attended
    gate = table_ref[pl.ds(ts_ref[0], 1), :]
    gate_ref[...] = gate
    scaled = (gate * cot_ref[0].astype(F32)).astype(BF16)
    p = lax.broadcasted_iota(jnp.int32, (HDM, 1), 0)
    part = p // 192
    inner = (p // 64) % 3
    half = (p // 32) % 2
    feature = (((p % 32) * 2 + (part ^ core)) * 2 + half) * 3 + inner
    pick = (lax.broadcasted_iota(jnp.int32, (HDM, HDM), 1) == feature).astype(F32).astype(BF16)
    picked = nt_dot(pick, attended).astype(BF16)
    for part, ref in ((0, keep_ref), (1, send_ref)):
        for yl in range(2):
            rows = [
                jnp.dot(
                    picked[((part * 3 + i) * 2 + yl) * 32 : ((part * 3 + i) * 2 + yl + 1) * 32],
                    scaled,
                    preferred_element_type=F32,
                ).astype(ref.dtype)
                for i in range(3)
            ]
            ref[yl * 4 + 0] = rows[0][:, :1152]
            ref[yl * 4 + 1, :, :384] = rows[0][:, 1152:]
            ref[yl * 4 + 1, :, 384:] = rows[1][:, :768]
            ref[yl * 4 + 2, :, :768] = rows[1][:, 768:]
            ref[yl * 4 + 2, :, 768:] = rows[2][:, :384]
            ref[yl * 4 + 3] = rows[2][:, 384:]


def mix_kernel(att_ref, here_ref, there_ref, own_ref, send_ref):
    core = lax.axis_index("c")
    rank = lax.axis_index("yh")
    attended = jnp.concatenate(
        [att_ref[pl.ds(rank * 64, 64), :], att_ref[pl.ds((1 - rank) * 64, 64), :]], axis=0
    )
    p = lax.broadcasted_iota(jnp.int32, (1, 256), 1)
    z, r = p // 8, p % 8
    rows = lax.broadcasted_iota(jnp.int32, (HDM, 256), 0)
    head = jnp.zeros((TOK, CHUNK), F32)
    tail = jnp.zeros((TOK, TAIL), F32)
    for part, ref in ((0, here_ref), (1, there_ref)):
        base = (z * 2 + (part ^ core)) * 6

        def expand(feature):
            pick = (rows == feature).astype(F32).astype(BF16)
            return jnp.dot(attended, pick, preferred_element_type=F32).astype(BF16)

        block = ref[...]
        left = expand(jnp.where(r < 6, base + r, -1))
        head = head + jnp.dot(left, block, preferred_element_type=F32)
        for s in range(3):
            right = expand(jnp.where(r >= 6, base + 3 * (r - 6) + s, -1))
            tail = tail + jnp.dot(
                right, block[:, s * TAIL : (s + 1) * TAIL], preferred_element_type=F32
            )
    own_ref[:, :CHUNK] = head[:64]
    own_ref[:, CHUNK:] = tail[:64]
    send_ref[:, :CHUNK] = head[64:].astype(BF16)
    send_ref[:, CHUNK:] = tail[64:].astype(BF16)


def fold_kernel(parts_ref, out_ref):
    total = jnp.sum(parts_ref[...].astype(F32), axis=0).astype(BF16)
    out_ref[:, 0, :] = total[:, :640]
    out_ref[:, 1, :512] = total[:, 640:]
    out_ref[:, 1, 512:] = jnp.zeros((ZS, 128), BF16)


def local(queries, keys, values, proj_weight, gate_table, timestep, span_index, cotangent):
    def call(kernel, shapes, flops=0, nbytes=0):
        return pl.pallas_call(
            kernel,
            out_shape=shapes,
            in_specs=None,
            out_specs=jax.tree.map(lambda _: VM, shapes),
            cost_estimate=pl.CostEstimate(flops=flops, bytes_accessed=nbytes, transcendentals=0),
        )

    S = jax.ShapeDtypeStruct
    swap = [(0, 1), (1, 0)]
    with jax.named_scope("kv"):
        pair = jnp.concatenate([keys[0], values[0]], axis=0)
        pair = jnp.broadcast_to(pair[None], (SPANS,) + pair.shape)
        pairs = lax.all_to_all(pair, SEQ, 0, 0, tiled=True)
    with jax.named_scope("wz"):
        copies = pl.pallas_call(
            spread_kernel,
            out_shape=S((ZS, 8, CHUNK), BF16),
            in_specs=[VM],
            out_specs=VM,
        )(proj_weight)
        here = lax.all_to_all(copies, "z", 0, 0, tiled=True)
    with jax.named_scope("attend"):
        keep, send, attended, gate = pl.pallas_call(
            attend_kernel,
            out_shape=(
                S((SPANS, ZS, CHUNK), F32),
                S((SPANS, ZS, CHUNK), BF16),
                S((TOK, HDM), BF16),
                S((1, WIDTH), F32),
            ),
            in_specs=[SM, SM, VM, VM, VM, VM],
            out_specs=(VM, VM, VM, VM),
        )(timestep, span_index, queries, pairs, cotangent, gate_table)
    with jax.named_scope("cores"):
        other = lax.ppermute(send, "c", swap)
    with jax.named_scope("plane"):
        both = (keep + other.astype(F32)).astype(BF16)
        parts = lax.all_to_all(both, SEQ, 0, 0, tiled=True)
    with jax.named_scope("fold"):
        slices = pl.pallas_call(
            fold_kernel,
            out_shape=S((ZS, 2, 640), BF16),
            in_specs=[VM],
            out_specs=VM,
        )(parts)
    with jax.named_scope("depth"):
        last = lax.all_to_all(slices, "z", 0, 0, tiled=True)
        total = jnp.sum(last.astype(F32), axis=0).reshape(1280)[:CHUNK]
        weight_grad = total.reshape(1, 9, 128)
    with jax.named_scope("wc"):
        there = lax.ppermute(here, "c", swap)
    with jax.named_scope("mix"):
        own, away = pl.pallas_call(
            mix_kernel,
            out_shape=(S((64, WIDTH), F32), S((64, WIDTH), BF16)),
            in_specs=[VM, VM, VM],
            out_specs=(VM, VM),
        )(attended, here.reshape(256, CHUNK), there.reshape(256, CHUNK))
    with jax.named_scope("mp"):
        near = lax.ppermute(away, "yh", swap)
        output = (gate * (own + near.astype(F32))).astype(BF16)[None]
    return output, weight_grad


def solution(mesh):
    grid = Mesh(mesh.devices.reshape(ZS, 2, 2, 4, 2), ("z", "c", "yl", "x", "yh"))
    dp = ("z", "c")
    return jax.shard_map(
        local,
        mesh=grid,
        in_specs=(
            P(dp, SEQ, "yh"),
            P(dp, SEQ, "yh"),
            P(dp, SEQ, "yh"),
            P("yh", dp, None),
            P(),
            P(dp),
            P(dp),
            P(dp, SEQ, None),
        ),
        out_specs=(P(dp, SEQ + ("yh",), None), P("yh", dp + SEQ, None)),
        check_vma=False,
    )
```

```python
import jax
import jax.numpy as jnp
from jax import lax
from jax.experimental import pallas as pl
from jax.experimental.pallas import tpu as pltpu
from jax.sharding import Mesh, PartitionSpec as P


HEAD = 128
TOK = 128
SPANS = 8
ZS = 32
WIDTH = 1536
HDM = 384
CHUNK = 1152
TAIL = WIDTH - CHUNK
SEQ = ("yl", "x")
F32 = jnp.float32
BF16 = jnp.bfloat16
VM = pl.BlockSpec(memory_space=pltpu.VMEM)
SM = pl.BlockSpec(memory_space=pltpu.SMEM)


def nt_dot(a, b):
    return lax.dot_general(a, b, (((1,), (1,)), ((), ())), preferred_element_type=F32)


def scale_kernel(ts_ref, cot_ref, table_ref, scaled_ref, gate_ref):
    gate = table_ref[pl.ds(ts_ref[0], 1), :]
    gate_ref[...] = gate
    scaled_ref[...] = (gate * cot_ref[0].astype(F32)).astype(BF16)


def attend_kernel(si_ref, q_ref, kv_ref, scaled_ref, keep_ref, send_ref, att_ref):
    place = lax.axis_index("yl") * 4 + lax.axis_index("x")
    core = lax.axis_index("c")
    limit = jnp.minimum(place, si_ref[0])
    inv_root = HEAD ** (-0.5)
    spans = lax.broadcasted_iota(jnp.int32, (1, SPANS * TOK), 1) // TOK
    visible = spans <= limit
    outs = []
    for h in range(HDM // HEAD):
        cols = slice(h * HEAD, (h + 1) * HEAD)
        keys = jnp.concatenate([kv_ref[j, :TOK, cols] for j in range(SPANS)], axis=0)
        values = jnp.concatenate([kv_ref[j, TOK:, cols] for j in range(SPANS)], axis=0)
        scores = nt_dot(q_ref[0, :, cols], keys) * inv_root
        scores = jnp.where(visible, scores, -jnp.inf)
        weights = jnp.exp(scores - jnp.max(scores, axis=1, keepdims=True))
        probs = (weights / jnp.sum(weights, axis=1, keepdims=True)).astype(BF16)
        outs.append(jnp.dot(probs, values, preferred_element_type=F32).astype(BF16))
    attended = jnp.concatenate(outs, axis=1)
    att_ref[...] = attended
    scaled = scaled_ref[...]
    p = lax.broadcasted_iota(jnp.int32, (HDM, 1), 0)
    part = p // 192
    inner = (p // 64) % 3
    half = (p // 32) % 2
    feature = (((p % 32) * 2 + (part ^ core)) * 2 + half) * 3 + inner
    pick = (lax.broadcasted_iota(jnp.int32, (HDM, HDM), 1) == feature).astype(F32).astype(BF16)
    picked = nt_dot(pick, attended).astype(BF16)
    for part, ref in ((0, keep_ref), (1, send_ref)):
        for yl in range(2):
            rows = [
                jnp.dot(
                    picked[((part * 3 + i) * 2 + yl) * 32 : ((part * 3 + i) * 2 + yl + 1) * 32],
                    scaled,
                    preferred_element_type=F32,
                ).astype(ref.dtype)
                for i in range(3)
            ]
            ref[yl * 4 + 0] = rows[0][:, :1152]
            ref[yl * 4 + 1, :, :384] = rows[0][:, 1152:]
            ref[yl * 4 + 1, :, 384:] = rows[1][:, :768]
            ref[yl * 4 + 2, :, :768] = rows[1][:, 768:]
            ref[yl * 4 + 2, :, 768:] = rows[2][:, :384]
            ref[yl * 4 + 3] = rows[2][:, 384:]


def merge_kernel(keep_ref, other_ref, near_ref, far_ref, out_ref):
    rows = jnp.concatenate([near_ref[...].astype(F32), far_ref[...].astype(F32)], axis=0)
    tails = [
        jnp.concatenate([rows[3 * q + s : 3 * q + s + 1, CHUNK:] for s in range(3)], axis=1)
        for q in range(8)
    ]
    block = jnp.concatenate([rows[:, :CHUNK]] + tails, axis=0).astype(BF16)
    for j in range(SPANS):
        out_ref[j, :ZS] = (keep_ref[j] + other_ref[j].astype(F32)).astype(BF16)
        out_ref[j, ZS:] = block


def expand_kernel(att_ref, out_ref):
    core = lax.axis_index("c")
    depth = lax.axis_index("z")
    attended = att_ref[...]
    p = lax.broadcasted_iota(jnp.int32, (1, 256), 1)
    place, r = p // 32, p % 32
    rows = lax.broadcasted_iota(jnp.int32, (HDM, 256), 0)
    for part in range(2):
        side = part ^ core
        for kind in range(4):
            row = r if kind == 0 else 3 * (r - 24) + kind - 1
            z = (depth + side * 8 + place - 8 + 16 * (row // 12) + ZS) % ZS
            t = row % 12
            feature = (z * 2 + ((t // 6) ^ side)) * 6 + t % 6
            feature = jnp.where((r < 24) == (kind == 0), feature, -1)
            pick = (rows == feature).astype(F32).astype(BF16)
            out_ref[part, kind] = jnp.dot(attended, pick, preferred_element_type=F32).astype(BF16)


def mix_kernel(wide_ref, here_ref, there_ref, own_ref, send_ref):
    rank = lax.axis_index("yh")
    head = jnp.zeros((TOK, CHUNK), F32)
    tail = jnp.zeros((TOK, TAIL), F32)
    for part, ref in ((0, here_ref), (1, there_ref)):
        block = ref[...].reshape(256, CHUNK)
        head = head + jnp.dot(wide_ref[part, 0], block, preferred_element_type=F32)
        for s in range(3):
            tail = tail + jnp.dot(
                wide_ref[part, 1 + s],
                block[:, s * TAIL : (s + 1) * TAIL],
                preferred_element_type=F32,
            )
    first = rank == 0
    for cols, m in ((slice(0, CHUNK), head), (slice(CHUNK, WIDTH), tail)):
        own_ref[:, cols] = jnp.where(first, m[:64], m[64:])
        send_ref[:, cols] = jnp.where(first, m[64:], m[:64]).astype(BF16)


def fold_kernel(parts_ref, out_ref, here_ref):
    total = parts_ref[0, :ZS].astype(F32)
    for j in range(1, SPANS):
        total = total + parts_ref[j, :ZS].astype(F32)
    total = total.astype(BF16)
    out_ref[:, 0, :] = total[:, :640]
    out_ref[:, 1, :512] = total[:, 640:]
    out_ref[:, 1, 512:] = jnp.zeros((ZS, 128), BF16)
    for j in range(SPANS):
        here_ref[j] = parts_ref[j, ZS:]


def columns(shift):
    pairs = []
    for z in range(ZS):
        for c in range(2):
            for s in range(SPANS):
                source = (z + c * 8 + s - 8 + shift) % ZS
                pairs.append(((source * 2 + c) * SPANS + s, (z * 2 + c) * SPANS + s))
    return pairs


def vmem(mib):
    return pltpu.CompilerParams(vmem_limit_bytes=mib << 20)


def local(queries, keys, values, proj_weight, gate_table, timestep, span_index, cotangent):
    S = jax.ShapeDtypeStruct
    swap = [(0, 1), (1, 0)]
    pair = jnp.concatenate([keys[0], values[0]], axis=0)
    pair = jnp.broadcast_to(pair[None], (SPANS,) + pair.shape)
    pairs = lax.all_to_all(pair, SEQ, 0, 0, tiled=True)
    every = ("z", "c") + SEQ
    mate = lax.ppermute(proj_weight[0], "c", swap)
    dozen = jnp.concatenate([proj_weight[0], mate], axis=0)
    far = lax.ppermute(dozen, every, columns(16))
    near = lax.ppermute(dozen, every, columns(0))
    scaled, gate = pl.pallas_call(
        scale_kernel,
        out_shape=(S((TOK, WIDTH), BF16), S((1, WIDTH), F32)),
        in_specs=[SM, VM, VM],
        out_specs=(VM, VM),
        compiler_params=vmem(8),
    )(timestep, cotangent, gate_table)
    keep, send, attended = pl.pallas_call(
        attend_kernel,
        out_shape=(S((SPANS, ZS, CHUNK), F32), S((SPANS, ZS, CHUNK), BF16), S((TOK, HDM), BF16)),
        in_specs=[SM, VM, VM, VM],
        out_specs=(VM, VM, VM),
        compiler_params=vmem(20),
    )(span_index, queries, pairs, scaled)
    other = lax.ppermute(send, "c", swap)
    both = pl.pallas_call(
        merge_kernel,
        out_shape=S((SPANS, 2 * ZS, CHUNK), BF16),
        in_specs=[VM, VM, VM, VM],
        out_specs=VM,
        compiler_params=vmem(8),
    )(keep, other, near, far)
    parts = lax.all_to_all(both, SEQ, 0, 0, tiled=True)
    wide = pl.pallas_call(
        expand_kernel,
        out_shape=S((2, 4, TOK, 256), BF16),
        in_specs=[VM],
        out_specs=VM,
        compiler_params=vmem(8),
    )(attended)
    slices, here = pl.pallas_call(
        fold_kernel,
        out_shape=(S((ZS, 2, 640), BF16), S((SPANS, ZS, CHUNK), BF16)),
        in_specs=[VM],
        out_specs=(VM, VM),
        compiler_params=vmem(8),
    )(parts)
    last = lax.all_to_all(slices, "z", 0, 0, tiled=True)
    total = jnp.sum(last.astype(F32), axis=0).reshape(1280)[:CHUNK]
    weight_grad = total.reshape(1, 9, 128)
    there = lax.ppermute(here, "c", swap)
    own, away = pl.pallas_call(
        mix_kernel,
        out_shape=(S((64, WIDTH), F32), S((64, WIDTH), BF16)),
        in_specs=[VM, VM, VM],
        out_specs=(VM, VM),
        compiler_params=vmem(12),
    )(wide, here, there)
    rest = lax.ppermute(away, "yh", swap)
    output = (gate * (own + rest.astype(F32))).astype(BF16)[None]
    return output, weight_grad


def solution(mesh):
    grid = Mesh(mesh.devices.reshape(ZS, 2, 2, 4, 2), ("z", "c", "yl", "x", "yh"))
    dp = ("z", "c")
    return jax.shard_map(
        local,
        mesh=grid,
        in_specs=(
            P(dp, SEQ, "yh"),
            P(dp, SEQ, "yh"),
            P(dp, SEQ, "yh"),
            P("yh", dp, None),
            P(),
            P(dp),
            P(dp),
            P(dp, SEQ, None),
        ),
        out_specs=(P(dp, SEQ + ("yh",), None), P("yh", dp + SEQ, None)),
        check_vma=False,
    )
```

```python
import jax
import jax.numpy as jnp
from jax import lax
from jax.experimental import pallas as pl
from jax.experimental.pallas import tpu as pltpu
from jax.sharding import Mesh, PartitionSpec as P


HEAD = 128
TOK = 128
SPANS = 8
ZS = 32
WIDTH = 1536
HDM = 384
CHUNK = 1152
SEQ = ("yl", "x")
F32 = jnp.float32
BF16 = jnp.bfloat16
VM = pl.BlockSpec(memory_space=pltpu.VMEM)
SM = pl.BlockSpec(memory_space=pltpu.SMEM)


def nt_dot(a, b):
    return lax.dot_general(a, b, (((1,), (1,)), ((), ())), preferred_element_type=F32)


def scale_kernel(ts_ref, cot_ref, table_ref, scaled_ref, gate_ref):
    gate = table_ref[pl.ds(ts_ref[0], 1), :]
    gate_ref[...] = gate
    scaled_ref[...] = (gate * cot_ref[0].astype(F32)).astype(BF16)


def attend_kernel(si_ref, q_ref, kv_ref, scaled_ref, keep_ref, send_ref, att_ref):
    place = lax.axis_index("yl") * 4 + lax.axis_index("x")
    core = lax.axis_index("c")
    limit = jnp.minimum(place, si_ref[0])
    inv_root = HEAD ** (-0.5)
    spans = lax.broadcasted_iota(jnp.int32, (1, SPANS * TOK), 1) // TOK
    visible = spans <= limit
    outs = []
    for h in range(HDM // HEAD):
        cols = slice(h * HEAD, (h + 1) * HEAD)
        keys = jnp.concatenate([kv_ref[j, :TOK, cols] for j in range(SPANS)], axis=0)
        values = jnp.concatenate([kv_ref[j, TOK:, cols] for j in range(SPANS)], axis=0)
        scores = nt_dot(q_ref[0, :, cols], keys) * inv_root
        scores = jnp.where(visible, scores, -jnp.inf)
        weights = jnp.exp(scores - jnp.max(scores, axis=1, keepdims=True))
        probs = (weights / jnp.sum(weights, axis=1, keepdims=True)).astype(BF16)
        outs.append(jnp.dot(probs, values, preferred_element_type=F32).astype(BF16))
    attended = jnp.concatenate(outs, axis=1)
    att_ref[...] = attended
    scaled = scaled_ref[...]
    p = lax.broadcasted_iota(jnp.int32, (HDM, 1), 0)
    part = p // 192
    inner = (p // 64) % 3
    half = (p // 32) % 2
    feature = (((p % 32) * 2 + (part ^ core)) * 2 + half) * 3 + inner
    pick = (lax.broadcasted_iota(jnp.int32, (HDM, HDM), 1) == feature).astype(F32).astype(BF16)
    picked = nt_dot(pick, attended).astype(BF16)
    for part, ref in ((0, keep_ref), (1, send_ref)):
        for yl in range(2):
            rows = [
                jnp.dot(
                    picked[((part * 3 + i) * 2 + yl) * 32 : ((part * 3 + i) * 2 + yl + 1) * 32],
                    scaled,
                    preferred_element_type=F32,
                ).astype(ref.dtype)
                for i in range(3)
            ]
            ref[yl * 4 + 0] = rows[0][:, :1152]
            ref[yl * 4 + 1, :, :384] = rows[0][:, 1152:]
            ref[yl * 4 + 1, :, 384:] = rows[1][:, :768]
            ref[yl * 4 + 2, :, :768] = rows[1][:, 768:]
            ref[yl * 4 + 2, :, 768:] = rows[2][:, :384]
            ref[yl * 4 + 3] = rows[2][:, 384:]


def pair_kernel(k_ref, v_ref, out_ref, sems):
    copies = []
    for j in range(SPANS):
        for i, ref in enumerate((k_ref, v_ref)):
            copies.append(
                pltpu.make_async_copy(
                    ref.at[0], out_ref.at[j, pl.ds(i * TOK, TOK), :], sems.at[2 * j + i]
                )
            )
    for copy in copies:
        copy.start()
    for copy in copies:
        copy.wait()


def expand_kernel(att_ref, out_ref):
    core = lax.axis_index("c")
    depth = lax.axis_index("z")
    x = lax.axis_index("x")
    yl = lax.axis_index("yl")
    attended = att_ref[...]
    p = lax.broadcasted_iota(jnp.int32, (1, 192), 1)
    place = (yl ^ ((p // 24) % 2)) * 4 + (x - p // 48 + 4) % 4
    half, t = (p // 12) % 2, p % 12
    rows = lax.broadcasted_iota(jnp.int32, (HDM, 192), 0)
    for part in range(2):
        side = part ^ core
        z = (depth + side * 8 + place - 8 + 16 * half + ZS) % ZS
        feature = (z * 2 + ((t // 6) ^ side)) * 6 + t % 6
        pick = (rows == feature).astype(F32).astype(BF16)
        out_ref[part] = jnp.dot(attended, pick, preferred_element_type=F32).astype(BF16)


def mix_kernel(wide_ref, here_ref, there_ref, own_ref, send_ref):
    mixed = jnp.dot(wide_ref[0], here_ref[...], preferred_element_type=F32)
    mixed = mixed + jnp.dot(wide_ref[1], there_ref[...], preferred_element_type=F32)
    first = lax.axis_index("yh") == 0
    own_ref[...] = jnp.where(first, mixed[:64], mixed[64:])
    send_ref[...] = jnp.where(first, mixed[64:], mixed[:64]).astype(BF16)


def add_kernel(keep_ref, other_ref, out_ref):
    out_ref[...] = (keep_ref[...] + other_ref[...].astype(F32)).astype(BF16)


def fold_kernel(parts_ref, out_ref):
    total = parts_ref[0].astype(F32)
    for j in range(1, SPANS):
        total = total + parts_ref[j].astype(F32)
    total = total.astype(BF16)
    out_ref[:, 0, :] = total[:, :640]
    out_ref[:, 1, :512] = total[:, 640:]
    out_ref[:, 1, 512:] = jnp.zeros((ZS, 128), BF16)


def sum_kernel(parts_ref, out_ref):
    total = jnp.sum(parts_ref[...].astype(F32), axis=0)
    for j in range(9):
        row, col = j // 5, (j % 5) * 128
        out_ref[j] = total[row : row + 1, col : col + 128]


def columns(shift):
    pairs = []
    for z in range(ZS):
        for c in range(2):
            for s in range(SPANS):
                source = (z + c * 8 + s - 8 + shift) % ZS
                pairs.append(((source * 2 + c) * SPANS + s, (z * 2 + c) * SPANS + s))
    return pairs


def vmem(mib):
    return pltpu.CompilerParams(vmem_limit_bytes=mib << 20)


def local(queries, keys, values, proj_weight, gate_table, timestep, span_index, cotangent):
    S = jax.ShapeDtypeStruct
    swap = [(0, 1), (1, 0)]
    pair = pl.pallas_call(
        pair_kernel,
        out_shape=S((SPANS, 2 * TOK, HDM), BF16),
        in_specs=[VM, VM],
        out_specs=pl.BlockSpec(memory_space=pl.ANY),
        scratch_shapes=[pltpu.SemaphoreType.DMA((2 * SPANS,))],
        compiler_params=vmem(4),
    )(keys, values)
    pairs = lax.all_to_all(pair, SEQ, 0, 0, tiled=True)
    every = ("z", "c") + SEQ
    mate = lax.ppermute(proj_weight[0], "c", swap)
    dozen = jnp.concatenate([proj_weight[0], mate], axis=0)
    far = lax.ppermute(dozen, every, columns(16))
    near = lax.ppermute(dozen, every, columns(0))
    scaled, gate = pl.pallas_call(
        scale_kernel,
        out_shape=(S((TOK, WIDTH), BF16), S((1, WIDTH), F32)),
        in_specs=[SM, VM, VM],
        out_specs=(VM, VM),
        compiler_params=vmem(8),
    )(timestep, cotangent, gate_table)
    keep, send, attended = pl.pallas_call(
        attend_kernel,
        out_shape=(
            S((SPANS, ZS, CHUNK), F32),
            S((SPANS, ZS, CHUNK), BF16),
            S((TOK, HDM), BF16),
        ),
        in_specs=[SM, VM, VM, VM],
        out_specs=(VM, VM, VM),
        compiler_params=vmem(20),
    )(span_index, queries, pairs, scaled)
    other = lax.ppermute(send, "c", swap)
    dozens = jnp.concatenate([near, far], axis=0)
    beside = lax.ppermute(dozens, "yl", swap)
    block = jnp.concatenate([dozens, beside], axis=0)
    both = pl.pallas_call(
        add_kernel,
        out_shape=S((SPANS, ZS, CHUNK), BF16),
        in_specs=[VM, VM],
        out_specs=VM,
        compiler_params=vmem(8),
    )(keep, other)
    parts = lax.all_to_all(both, SEQ, 0, 0, tiled=True)
    wide = pl.pallas_call(
        expand_kernel,
        out_shape=S((2, TOK, 192), BF16),
        in_specs=[VM],
        out_specs=VM,
        compiler_params=vmem(8),
    )(attended)
    blocks = [block]
    for k in range(1, 4):
        blocks.append(lax.ppermute(block, "x", [(i, (i + k) % 4) for i in range(4)]))
    slices = pl.pallas_call(
        fold_kernel,
        out_shape=S((ZS, 2, 640), BF16),
        in_specs=[VM],
        out_specs=VM,
        compiler_params=vmem(8),
    )(parts)
    last = lax.all_to_all(slices, "z", 0, 0, tiled=True)
    weight_grad = pl.pallas_call(
        sum_kernel,
        out_shape=S((9, 1, 128), F32),
        in_specs=[VM],
        out_specs=VM,
        compiler_params=vmem(8),
    )(last).reshape(1, 9, 128)
    here = jnp.concatenate(blocks, axis=0)
    there = lax.ppermute(here, "c", swap)
    own, away = pl.pallas_call(
        mix_kernel,
        out_shape=(S((64, WIDTH), F32), S((64, WIDTH), BF16)),
        in_specs=[VM, VM, VM],
        out_specs=(VM, VM),
        compiler_params=vmem(12),
    )(wide, here, there)
    rest = lax.ppermute(away, "yh", swap)
    output = (gate * (own + rest.astype(F32))).astype(BF16)[None]
    return output, weight_grad


def solution(mesh):
    grid = Mesh(mesh.devices.reshape(ZS, 2, 2, 4, 2), ("z", "c", "yl", "x", "yh"))
    dp = ("z", "c")
    return jax.shard_map(
        local,
        mesh=grid,
        in_specs=(
            P(dp, SEQ, "yh"),
            P(dp, SEQ, "yh"),
            P(dp, SEQ, "yh"),
            P("yh", dp, None),
            P(),
            P(dp),
            P(dp),
            P(dp, SEQ, None),
        ),
        out_specs=(P(dp, SEQ + ("yh",), None), P("yh", dp + SEQ, None)),
        check_vma=False,
    )
```

```python
import jax
import jax.numpy as jnp
from jax import lax
from jax.experimental import pallas as pl
from jax.experimental.pallas import tpu as pltpu
from jax.sharding import Mesh, PartitionSpec as P


HEAD = 128
TOK = 128
SPANS = 8
ZS = 32
WIDTH = 1536
HDM = 384
CHUNK = 1152
SEQ = ("yl", "x")
F32 = jnp.float32
BF16 = jnp.bfloat16
VM = pl.BlockSpec(memory_space=pltpu.VMEM)
SM = pl.BlockSpec(memory_space=pltpu.SMEM)


def nt_dot(a, b):
    return lax.dot_general(a, b, (((1,), (1,)), ((), ())), preferred_element_type=F32)


def scale_kernel(ts_ref, cot_ref, table_ref, scaled_ref, gate_ref):
    gate = table_ref[pl.ds(ts_ref[0], 1), :]
    gate_ref[...] = gate
    scaled_ref[...] = (gate * cot_ref[0].astype(F32)).astype(BF16)


def attend_kernel(si_ref, q_ref, kv_ref, scaled_ref, keep_ref, send_ref, att_ref):
    place = lax.axis_index("yl") * 4 + lax.axis_index("x")
    core = lax.axis_index("c")
    limit = jnp.minimum(place, si_ref[0])
    inv_root = HEAD ** (-0.5)
    spans = lax.broadcasted_iota(jnp.int32, (1, SPANS * TOK), 1) // TOK
    visible = spans <= limit
    outs = []
    for h in range(HDM // HEAD):
        cols = slice(h * HEAD, (h + 1) * HEAD)
        keys = jnp.concatenate([kv_ref[j, :TOK, cols] for j in range(SPANS)], axis=0)
        values = jnp.concatenate([kv_ref[j, TOK:, cols] for j in range(SPANS)], axis=0)
        scores = nt_dot(q_ref[0, :, cols], keys) * inv_root
        scores = jnp.where(visible, scores, -jnp.inf)
        weights = jnp.exp(scores - jnp.max(scores, axis=1, keepdims=True))
        probs = (weights / jnp.sum(weights, axis=1, keepdims=True)).astype(BF16)
        outs.append(jnp.dot(probs, values, preferred_element_type=F32).astype(BF16))
    attended = jnp.concatenate(outs, axis=1)
    att_ref[...] = attended
    scaled = scaled_ref[...]
    p = lax.broadcasted_iota(jnp.int32, (HDM, 1), 0)
    part = p // 192
    inner = (p // 64) % 3
    half = (p // 32) % 2
    feature = (((p % 32) * 2 + (part ^ core)) * 2 + half) * 3 + inner
    pick = (lax.broadcasted_iota(jnp.int32, (HDM, HDM), 1) == feature).astype(F32).astype(BF16)
    picked = nt_dot(pick, attended).astype(BF16)
    for part, ref in ((0, keep_ref), (1, send_ref)):
        for yl in range(2):
            rows = [
                jnp.dot(
                    picked[((part * 3 + i) * 2 + yl) * 32 : ((part * 3 + i) * 2 + yl + 1) * 32],
                    scaled,
                    preferred_element_type=F32,
                ).astype(ref.dtype)
                for i in range(3)
            ]
            ref[yl * 4 + 0] = rows[0][:, :1152]
            ref[yl * 4 + 1, :, :384] = rows[0][:, 1152:]
            ref[yl * 4 + 1, :, 384:] = rows[1][:, :768]
            ref[yl * 4 + 2, :, :768] = rows[1][:, 768:]
            ref[yl * 4 + 2, :, 768:] = rows[2][:, :384]
            ref[yl * 4 + 3] = rows[2][:, 384:]


def pair_kernel(k_ref, v_ref, out_ref, held, in_sems, sems):
    loads = [
        pltpu.make_async_copy(ref.at[0], held.at[i], in_sems.at[i])
        for i, ref in enumerate((k_ref, v_ref))
    ]
    for load in loads:
        load.start()
    copies = []
    for i, load in enumerate(loads):
        load.wait()
        for j in range(SPANS):
            copy = pltpu.make_async_copy(
                held.at[i], out_ref.at[j, pl.ds(i * TOK, TOK), :], sems.at[i * SPANS + j]
            )
            copy.start()
            copies.append(copy)
    for copy in copies:
        copy.wait()


def expand_kernel(att_ref, out_ref):
    core = lax.axis_index("c")
    depth = lax.axis_index("z")
    x = lax.axis_index("x")
    yl = lax.axis_index("yl")
    attended = att_ref[...]
    p = lax.broadcasted_iota(jnp.int32, (1, 192), 1)
    place = (yl ^ ((p // 24) % 2)) * 4 + (x - p // 48 + 4) % 4
    half, t = (p // 12) % 2, p % 12
    rows = lax.broadcasted_iota(jnp.int32, (HDM, 192), 0)
    for part in range(2):
        side = part ^ core
        z = (depth + side * 8 + place - 8 + 16 * half + ZS) % ZS
        feature = (z * 2 + ((t // 6) ^ side)) * 6 + t % 6
        pick = (rows == feature).astype(F32).astype(BF16)
        out_ref[part] = jnp.dot(attended, pick, preferred_element_type=F32).astype(BF16)


def mix_kernel(wide_ref, here_ref, there_ref, own_ref, send_ref):
    mixed = jnp.dot(wide_ref[0], here_ref[...], preferred_element_type=F32)
    mixed = mixed + jnp.dot(wide_ref[1], there_ref[...], preferred_element_type=F32)
    first = lax.axis_index("yh") == 0
    own_ref[...] = jnp.where(first, mixed[:64], mixed[64:])
    send_ref[...] = jnp.where(first, mixed[64:], mixed[:64]).astype(BF16)


def add_kernel(keep_ref, other_ref, out_ref):
    out_ref[...] = (keep_ref[...] + other_ref[...].astype(F32)).astype(BF16)


def fold_kernel(parts_ref, out_ref):
    total = parts_ref[0].astype(F32)
    for j in range(1, SPANS):
        total = total + parts_ref[j].astype(F32)
    total = total.astype(BF16)
    out_ref[:, 0, :] = total[:, :640]
    out_ref[:, 1, :512] = total[:, 640:]
    out_ref[:, 1, 512:] = jnp.zeros((ZS, 128), BF16)


def sum_kernel(parts_ref, out_ref):
    total = jnp.sum(parts_ref[...].astype(F32), axis=0)
    for j in range(9):
        row, col = j // 5, (j % 5) * 128
        out_ref[j] = total[row : row + 1, col : col + 128]


def columns(shift):
    pairs = []
    for z in range(ZS):
        for c in range(2):
            for s in range(SPANS):
                source = (z + c * 8 + s - 8 + shift) % ZS
                pairs.append(((source * 2 + c) * SPANS + s, (z * 2 + c) * SPANS + s))
    return pairs


def vmem(mib):
    return pltpu.CompilerParams(vmem_limit_bytes=mib << 20)


def local(queries, keys, values, proj_weight, gate_table, timestep, span_index, cotangent):
    S = jax.ShapeDtypeStruct
    swap = [(0, 1), (1, 0)]
    pair = pl.pallas_call(
        pair_kernel,
        out_shape=S((SPANS, 2 * TOK, HDM), BF16),
        in_specs=[pl.BlockSpec(memory_space=pltpu.HBM)] * 2,
        out_specs=pl.BlockSpec(memory_space=pl.ANY),
        scratch_shapes=[
            pltpu.VMEM((2, TOK, HDM), BF16),
            pltpu.SemaphoreType.DMA((2,)),
            pltpu.SemaphoreType.DMA((2 * SPANS,)),
        ],
        compiler_params=pltpu.CompilerParams(vmem_limit_bytes=67043328),
    )(keys, values)
    pairs = lax.all_to_all(pair, SEQ, 0, 0, tiled=True)
    every = ("z", "c") + SEQ
    mate = lax.ppermute(proj_weight[0], "c", swap)
    dozen = jnp.concatenate([proj_weight[0], mate], axis=0)
    far = lax.ppermute(dozen, every, columns(16))
    near = lax.ppermute(dozen, every, columns(0))
    scaled, gate = pl.pallas_call(
        scale_kernel,
        out_shape=(S((TOK, WIDTH), BF16), S((1, WIDTH), F32)),
        in_specs=[SM, VM, VM],
        out_specs=(VM, VM),
        compiler_params=vmem(8),
    )(timestep, cotangent, gate_table)
    keep, send, attended = pl.pallas_call(
        attend_kernel,
        out_shape=(
            S((SPANS, ZS, CHUNK), F32),
            S((SPANS, ZS, CHUNK), BF16),
            S((TOK, HDM), BF16),
        ),
        in_specs=[SM, VM, VM, VM],
        out_specs=(VM, VM, VM),
        compiler_params=vmem(20),
    )(span_index, queries, pairs, scaled)
    other = lax.ppermute(send, "c", swap)
    dozens = jnp.concatenate([near, far], axis=0)
    beside = lax.ppermute(dozens, "yl", swap)
    block = jnp.concatenate([dozens, beside], axis=0)
    both = pl.pallas_call(
        add_kernel,
        out_shape=S((SPANS, ZS, CHUNK), BF16),
        in_specs=[VM, VM],
        out_specs=VM,
        compiler_params=vmem(8),
    )(keep, other)
    parts = lax.all_to_all(both, SEQ, 0, 0, tiled=True)
    wide = pl.pallas_call(
        expand_kernel,
        out_shape=S((2, TOK, 192), BF16),
        in_specs=[VM],
        out_specs=VM,
        compiler_params=vmem(8),
    )(attended)
    blocks = [block]
    for k in range(1, 4):
        blocks.append(lax.ppermute(block, "x", [(i, (i + k) % 4) for i in range(4)]))
    slices = pl.pallas_call(
        fold_kernel,
        out_shape=S((ZS, 2, 640), BF16),
        in_specs=[VM],
        out_specs=VM,
        compiler_params=vmem(8),
    )(parts)
    last = lax.all_to_all(slices, "z", 0, 0, tiled=True)
    weight_grad = pl.pallas_call(
        sum_kernel,
        out_shape=S((9, 1, 128), F32),
        in_specs=[VM],
        out_specs=VM,
        compiler_params=vmem(8),
    )(last).reshape(1, 9, 128)
    here = jnp.concatenate(blocks, axis=0)
    there = lax.ppermute(here, "c", swap)
    own, away = pl.pallas_call(
        mix_kernel,
        out_shape=(S((64, WIDTH), F32), S((64, WIDTH), BF16)),
        in_specs=[VM, VM, VM],
        out_specs=(VM, VM),
        compiler_params=vmem(12),
    )(wide, here, there)
    rest = lax.ppermute(away, "yh", swap)
    output = (gate * (own + rest.astype(F32))).astype(BF16)[None]
    return output, weight_grad


def solution(mesh):
    grid = Mesh(mesh.devices.reshape(ZS, 2, 2, 4, 2), ("z", "c", "yl", "x", "yh"))
    dp = ("z", "c")
    return jax.shard_map(
        local,
        mesh=grid,
        in_specs=(
            P(dp, SEQ, "yh"),
            P(dp, SEQ, "yh"),
            P(dp, SEQ, "yh"),
            P("yh", dp, None),
            P(),
            P(dp),
            P(dp),
            P(dp, SEQ, None),
        ),
        out_specs=(P(dp, SEQ + ("yh",), None), P("yh", dp + SEQ, None)),
        check_vma=False,
    )
```

```python
import jax
import jax.numpy as jnp
from jax import lax
from jax.experimental import pallas as pl
from jax.experimental.pallas import tpu as pltpu
from jax.sharding import Mesh, PartitionSpec as P


HEAD = 128
TOK = 128
SPANS = 8
ZS = 32
WIDTH = 1536
HDM = 384
CHUNK = 1152
TAIL = WIDTH - CHUNK
SEQ = ("yl", "x")
F32 = jnp.float32
BF16 = jnp.bfloat16
VM = pl.BlockSpec(memory_space=pltpu.VMEM)


def nt_dot(a, b):
    return lax.dot_general(a, b, (((1,), (1,)), ((), ())), preferred_element_type=F32)


def pack_kernel(own_ref, mate_ref, out_ref):
    rows = jnp.concatenate([own_ref[0].astype(F32), mate_ref[...].astype(F32)], axis=0)
    tails = [
        jnp.concatenate([rows[3 * q + s : 3 * q + s + 1, CHUNK:] for s in range(3)], axis=1)
        for q in range(4)
    ]
    out_ref[...] = jnp.concatenate([rows[:, :CHUNK]] + tails, axis=0).astype(BF16)


def scale_kernel(ts_ref, si_ref, cot_ref, table_ref, scaled_ref, gate_ref, bias_ref):
    place = lax.axis_index("yl") * 4 + lax.axis_index("x")
    spans = lax.broadcasted_iota(jnp.int32, (1, SPANS * TOK), 1) // TOK
    bias_ref[...] = jnp.where(spans <= jnp.minimum(si_ref[...], place), 0.0, -jnp.inf)
    step_hit = lax.broadcasted_iota(jnp.int32, (4, 1), 0) == ts_ref[...]
    gate = jnp.sum(jnp.where(step_hit, table_ref[...], 0.0), axis=0, keepdims=True)
    gate_ref[...] = gate
    scaled_ref[...] = (gate * cot_ref[0].astype(F32)).astype(BF16)


def attend_kernel(q_ref, kv_ref, scaled_ref, bias_ref, keep_ref, send_ref, att_ref):
    core = lax.axis_index("c")
    inv_root = HEAD ** (-0.5)
    bias = bias_ref[...]
    outs = []
    for h in range(HDM // HEAD):
        cols = slice(h * HEAD, (h + 1) * HEAD)
        keys = jnp.concatenate([kv_ref[j, :TOK, cols] for j in range(SPANS)], axis=0)
        values = jnp.concatenate([kv_ref[j, TOK:, cols] for j in range(SPANS)], axis=0)
        scores = nt_dot(q_ref[0, :, cols], keys) * inv_root + bias
        weights = jnp.exp(scores - jnp.max(scores, axis=1, keepdims=True))
        probs = (weights / jnp.sum(weights, axis=1, keepdims=True)).astype(BF16)
        outs.append(jnp.dot(probs, values, preferred_element_type=F32).astype(BF16))
    attended = jnp.concatenate(outs, axis=1)
    att_ref[...] = attended
    scaled = scaled_ref[...]
    p = lax.broadcasted_iota(jnp.int32, (HDM, 1), 0)
    part = p // 192
    inner = (p // 64) % 3
    half = (p // 32) % 2
    feature = (((p % 32) * 2 + (part ^ core)) * 2 + half) * 3 + inner
    pick = (lax.broadcasted_iota(jnp.int32, (HDM, HDM), 1) == feature).astype(F32).astype(BF16)
    picked = nt_dot(pick, attended).astype(BF16)
    for part, ref in ((0, keep_ref), (1, send_ref)):
        for yl in range(2):
            rows = [
                jnp.dot(
                    picked[((part * 3 + i) * 2 + yl) * 32 : ((part * 3 + i) * 2 + yl + 1) * 32],
                    scaled,
                    preferred_element_type=F32,
                ).astype(ref.dtype)
                for i in range(3)
            ]
            ref[yl * 4 + 0] = rows[0][:, :1152]
            ref[yl * 4 + 1, :, :384] = rows[0][:, 1152:]
            ref[yl * 4 + 1, :, 384:] = rows[1][:, :768]
            ref[yl * 4 + 2, :, :768] = rows[1][:, 768:]
            ref[yl * 4 + 2, :, 768:] = rows[2][:, :384]
            ref[yl * 4 + 3] = rows[2][:, 384:]


def pair_kernel(k_ref, v_ref, out_ref, held, in_sems, sems):
    loads = [
        pltpu.make_async_copy(ref.at[0], held.at[i], in_sems.at[i])
        for i, ref in enumerate((k_ref, v_ref))
    ]
    for load in loads:
        load.start()
    copies = []
    for i, load in enumerate(loads):
        load.wait()
        for j in range(SPANS):
            copy = pltpu.make_async_copy(
                held.at[i], out_ref.at[j, pl.ds(i * TOK, TOK), :], sems.at[i * SPANS + j]
            )
            copy.start()
            copies.append(copy)
    for copy in copies:
        copy.wait()


def merge_kernel(keep_ref, other_ref, near_ref, far_ref, out_ref):
    near, far = near_ref[...], far_ref[...]
    for j in range(SPANS):
        out_ref[j, :ZS] = (keep_ref[j] + other_ref[j].astype(F32)).astype(BF16)
        out_ref[j, ZS : ZS + 16] = near
        out_ref[j, ZS + 16 :] = far


def expand_kernel(att_ref, out_ref):
    core = lax.axis_index("c")
    depth = lax.axis_index("z")
    attended = att_ref[...]
    p = lax.broadcasted_iota(jnp.int32, (1, 256), 1)
    place, r = p // 32, p % 32
    rows = lax.broadcasted_iota(jnp.int32, (HDM, 256), 0)
    for part in range(2):
        side = part ^ core
        for kind in range(4):
            row = r % 16
            t = row if kind == 0 else 3 * (row - 12) + kind - 1
            z = (depth + side * 8 + place - 8 + 16 * (r // 16) + ZS) % ZS
            feature = (z * 2 + ((t // 6) ^ side)) * 6 + t % 6
            feature = jnp.where((row < 12) == (kind == 0), feature, -1)
            pick = (rows == feature).astype(F32).astype(BF16)
            out_ref[part, kind] = jnp.dot(attended, pick, preferred_element_type=F32).astype(BF16)


def mix_kernel(wide_ref, here_ref, there_ref, own_ref, send_ref):
    rank = lax.axis_index("yh")
    head = jnp.zeros((TOK, CHUNK), F32)
    tail = jnp.zeros((TOK, TAIL), F32)
    for part, ref in ((0, here_ref), (1, there_ref)):
        block = ref[...].reshape(256, CHUNK)
        head = head + jnp.dot(wide_ref[part, 0], block, preferred_element_type=F32)
        for s in range(3):
            tail = tail + jnp.dot(
                wide_ref[part, 1 + s],
                block[:, s * TAIL : (s + 1) * TAIL],
                preferred_element_type=F32,
            )
    first = rank == 0
    for cols, m in ((slice(0, CHUNK), head), (slice(CHUNK, WIDTH), tail)):
        own_ref[:, cols] = jnp.where(first, m[:64], m[64:])
        send_ref[:, cols] = jnp.where(first, m[64:], m[:64]).astype(BF16)


def fold_kernel(parts_ref, out_ref, here_ref):
    total = parts_ref[0, :ZS].astype(F32)
    for j in range(1, SPANS):
        total = total + parts_ref[j, :ZS].astype(F32)
    total = total.astype(BF16)
    out_ref[:, 0, :] = total[:, :640]
    out_ref[:, 1, :512] = total[:, 640:]
    out_ref[:, 1, 512:] = jnp.zeros((ZS, 128), BF16)
    for j in range(SPANS):
        here_ref[j] = parts_ref[j, ZS:]


def sum_kernel(parts_ref, out_ref):
    total = jnp.sum(parts_ref[...].astype(F32), axis=0)
    for j in range(9):
        row, col = j // 5, (j % 5) * 128
        out_ref[j] = total[row : row + 1, col : col + 128]


def columns(shift):
    pairs = []
    for z in range(ZS):
        for c in range(2):
            for s in range(SPANS):
                source = (z + c * 8 + s - 8 + shift) % ZS
                pairs.append(((source * 2 + c) * SPANS + s, (z * 2 + c) * SPANS + s))
    return pairs


def vmem(mib):
    return pltpu.CompilerParams(vmem_limit_bytes=mib << 20)


def local(queries, keys, values, proj_weight, gate_table, timestep, span_index, cotangent):
    S = jax.ShapeDtypeStruct
    swap = [(0, 1), (1, 0)]
    pair = pl.pallas_call(
        pair_kernel,
        out_shape=S((SPANS, 2 * TOK, HDM), BF16),
        in_specs=[pl.BlockSpec(memory_space=pltpu.HBM)] * 2,
        out_specs=pl.BlockSpec(memory_space=pl.ANY),
        scratch_shapes=[
            pltpu.VMEM((2, TOK, HDM), BF16),
            pltpu.SemaphoreType.DMA((2,)),
            pltpu.SemaphoreType.DMA((2 * SPANS,)),
        ],
        compiler_params=pltpu.CompilerParams(vmem_limit_bytes=67043328),
    )(keys, values)
    pairs = lax.all_to_all(pair, SEQ, 0, 0, tiled=True)
    every = ("z", "c") + SEQ
    mate = lax.ppermute(proj_weight[0], "c", swap)
    dozen = pl.pallas_call(
        pack_kernel,
        out_shape=S((16, CHUNK), BF16),
        in_specs=[VM, VM],
        out_specs=VM,
        compiler_params=vmem(8),
    )(proj_weight, mate)
    far = lax.ppermute(dozen, every, columns(16))
    near = lax.ppermute(dozen, every, columns(0))
    scaled, gate, bias = pl.pallas_call(
        scale_kernel,
        out_shape=(S((TOK, WIDTH), BF16), S((1, WIDTH), F32), S((1, SPANS * TOK), F32)),
        in_specs=[VM, VM, VM, VM],
        out_specs=(VM, VM, VM),
        compiler_params=vmem(8),
    )(timestep.reshape(1, 1), span_index.reshape(1, 1), cotangent, gate_table)
    keep, send, attended = pl.pallas_call(
        attend_kernel,
        out_shape=(S((SPANS, ZS, CHUNK), F32), S((SPANS, ZS, CHUNK), BF16), S((TOK, HDM), BF16)),
        in_specs=[VM, VM, VM, VM],
        out_specs=(VM, VM, VM),
        compiler_params=vmem(20),
    )(queries, pairs, scaled, bias)
    other = lax.ppermute(send, "c", swap)
    both = pl.pallas_call(
        merge_kernel,
        out_shape=S((SPANS, 2 * ZS, CHUNK), BF16),
        in_specs=[VM, VM, VM, VM],
        out_specs=VM,
        compiler_params=vmem(8),
    )(keep, other, near, far)
    parts = lax.all_to_all(both, SEQ, 0, 0, tiled=True)
    wide = pl.pallas_call(
        expand_kernel,
        out_shape=S((2, 4, TOK, 256), BF16),
        in_specs=[VM],
        out_specs=VM,
        compiler_params=vmem(8),
    )(attended)
    slices, here = pl.pallas_call(
        fold_kernel,
        out_shape=(S((ZS, 2, 640), BF16), S((SPANS, ZS, CHUNK), BF16)),
        in_specs=[VM],
        out_specs=(VM, VM),
        compiler_params=vmem(8),
    )(parts)
    last = lax.all_to_all(slices, "z", 0, 0, tiled=True)
    weight_grad = pl.pallas_call(
        sum_kernel,
        out_shape=S((9, 1, 128), F32),
        in_specs=[VM],
        out_specs=VM,
        compiler_params=vmem(8),
    )(last).reshape(1, 9, 128)
    there = lax.ppermute(here, "c", swap)
    own, away = pl.pallas_call(
        mix_kernel,
        out_shape=(S((64, WIDTH), F32), S((64, WIDTH), BF16)),
        in_specs=[VM, VM, VM],
        out_specs=(VM, VM),
        compiler_params=vmem(12),
    )(wide, here, there)
    rest = lax.ppermute(away, "yh", swap)
    output = (gate * (own + rest.astype(F32))).astype(BF16)[None]
    return output, weight_grad


def solution(mesh):
    grid = Mesh(mesh.devices.reshape(ZS, 2, 2, 4, 2), ("z", "c", "yl", "x", "yh"))
    dp = ("z", "c")
    return jax.shard_map(
        local,
        mesh=grid,
        in_specs=(
            P(dp, SEQ, "yh"),
            P(dp, SEQ, "yh"),
            P(dp, SEQ, "yh"),
            P("yh", dp, None),
            P(),
            P(dp),
            P(dp),
            P(dp, SEQ, None),
        ),
        out_specs=(P(dp, SEQ + ("yh",), None), P("yh", dp + SEQ, None)),
        check_vma=False,
    )
```

```python
import jax
import jax.numpy as jnp
from jax import lax
from jax.experimental import pallas as pl
from jax.experimental.pallas import tpu as pltpu
from jax.sharding import Mesh, PartitionSpec as P


HEAD = 128
TOK = 128
SPANS = 8
ZS = 32
WIDTH = 1536
HDM = 384
CHUNK = 1152
TAIL = WIDTH - CHUNK
SEQ = ("yl", "x")
F32 = jnp.float32
BF16 = jnp.bfloat16
VM = pl.BlockSpec(memory_space=pltpu.VMEM)


def nt_dot(a, b):
    return lax.dot_general(a, b, (((1,), (1,)), ((), ())), preferred_element_type=F32)


def pack_kernel(own_ref, mate_ref, out_ref):
    rows = jnp.concatenate([own_ref[0].astype(F32), mate_ref[...].astype(F32)], axis=0)
    tails = [
        jnp.concatenate([rows[3 * q + s : 3 * q + s + 1, CHUNK:] for s in range(3)], axis=1)
        for q in range(4)
    ]
    out_ref[...] = jnp.concatenate([rows[:, :CHUNK]] + tails, axis=0).astype(BF16)


def scale_kernel(ts_ref, si_ref, cot_ref, table_ref, scaled_ref, gate_ref, bias_ref):
    place = lax.axis_index("yl") * 4 + lax.axis_index("x")
    spans = lax.broadcasted_iota(jnp.int32, (1, SPANS * TOK), 1) // TOK
    bias_ref[...] = jnp.where(spans <= jnp.minimum(si_ref[...], place), 0.0, -jnp.inf)
    step_hit = lax.broadcasted_iota(jnp.int32, (4, 1), 0) == ts_ref[...]
    gate = jnp.sum(jnp.where(step_hit, table_ref[...], 0.0), axis=0, keepdims=True)
    gate_ref[...] = gate
    scaled_ref[...] = (gate * cot_ref[0].astype(F32)).astype(BF16)


def attend_kernel(q_ref, kv_ref, scaled_ref, bias_ref, keep_ref, send_ref, att_ref):
    core = lax.axis_index("c")
    inv_root = HEAD ** (-0.5)
    bias = bias_ref[...]
    outs = []
    for h in range(HDM // HEAD):
        cols = slice(h * HEAD, (h + 1) * HEAD)
        keys = jnp.concatenate([kv_ref[j, :TOK, cols] for j in range(SPANS)], axis=0)
        values = jnp.concatenate([kv_ref[j, TOK:, cols] for j in range(SPANS)], axis=0)
        scores = nt_dot(q_ref[0, :, cols], keys) * inv_root + bias
        weights = jnp.exp(scores - jnp.max(scores, axis=1, keepdims=True))
        probs = (weights * (1.0 / jnp.sum(weights, axis=1, keepdims=True))).astype(BF16)
        outs.append(jnp.dot(probs, values, preferred_element_type=F32).astype(BF16))
    attended = jnp.concatenate(outs, axis=1)
    att_ref[...] = attended
    scaled = scaled_ref[...]
    p = lax.broadcasted_iota(jnp.int32, (HDM, 1), 0)
    part = p // 192
    inner = (p // 64) % 3
    half = (p // 32) % 2
    feature = (((p % 32) * 2 + (part ^ core)) * 2 + half) * 3 + inner
    pick = (lax.broadcasted_iota(jnp.int32, (HDM, HDM), 1) == feature).astype(F32).astype(BF16)
    picked = nt_dot(pick, attended).astype(BF16)
    for part, ref in ((0, keep_ref), (1, send_ref)):
        for yl in range(2):
            rows = [
                jnp.dot(
                    picked[((part * 3 + i) * 2 + yl) * 32 : ((part * 3 + i) * 2 + yl + 1) * 32],
                    scaled,
                    preferred_element_type=F32,
                ).astype(ref.dtype)
                for i in range(3)
            ]
            ref[yl * 4 + 0] = rows[0][:, :1152]
            ref[yl * 4 + 1, :, :384] = rows[0][:, 1152:]
            ref[yl * 4 + 1, :, 384:] = rows[1][:, :768]
            ref[yl * 4 + 2, :, :768] = rows[1][:, 768:]
            ref[yl * 4 + 2, :, 768:] = rows[2][:, :384]
            ref[yl * 4 + 3] = rows[2][:, 384:]


def pair_kernel(k_ref, v_ref, out_ref, held, in_sems, sems):
    loads = [
        pltpu.make_async_copy(ref.at[0], held.at[i], in_sems.at[i])
        for i, ref in enumerate((k_ref, v_ref))
    ]
    for load in loads:
        load.start()
    copies = []
    for i, load in enumerate(loads):
        load.wait()
        for j in range(SPANS):
            copy = pltpu.make_async_copy(
                held.at[i], out_ref.at[j, pl.ds(i * TOK, TOK), :], sems.at[i * SPANS + j]
            )
            copy.start()
            copies.append(copy)
    for copy in copies:
        copy.wait()


def add_kernel(keep_ref, other_ref, out_ref):
    out_ref[...] = (keep_ref[...] + other_ref[...].astype(F32)).astype(BF16)


def expand_kernel(att_ref, out_ref):
    core = lax.axis_index("c")
    depth = lax.axis_index("z")
    attended = att_ref[...]
    x, yl = lax.axis_index("x"), lax.axis_index("yl")
    p = lax.broadcasted_iota(jnp.int32, (1, 256), 1)
    place = (yl ^ ((p // 32) % 2)) * 4 + (x - p // 64 + 4) % 4
    r = p % 32
    rows = lax.broadcasted_iota(jnp.int32, (HDM, 256), 0)
    for part in range(2):
        side = part ^ core
        for kind in range(4):
            row = r % 16
            t = row if kind == 0 else 3 * (row - 12) + kind - 1
            z = (depth + side * 8 + place - 8 + 16 * (r // 16) + ZS) % ZS
            feature = (z * 2 + ((t // 6) ^ side)) * 6 + t % 6
            feature = jnp.where((row < 12) == (kind == 0), feature, -1)
            pick = (rows == feature).astype(F32).astype(BF16)
            out_ref[part, kind] = jnp.dot(attended, pick, preferred_element_type=F32).astype(BF16)


def mix_kernel(wide_ref, here_ref, there_ref, own_ref, send_ref):
    rank = lax.axis_index("yh")
    head = jnp.zeros((TOK, CHUNK), F32)
    tail = jnp.zeros((TOK, TAIL), F32)
    for part, ref in ((0, here_ref), (1, there_ref)):
        block = ref[...]
        head = head + jnp.dot(wide_ref[part, 0], block, preferred_element_type=F32)
        for s in range(3):
            tail = tail + jnp.dot(
                wide_ref[part, 1 + s],
                block[:, s * TAIL : (s + 1) * TAIL],
                preferred_element_type=F32,
            )
    first = rank == 0
    for cols, m in ((slice(0, CHUNK), head), (slice(CHUNK, WIDTH), tail)):
        own_ref[:, cols] = jnp.where(first, m[:64], m[64:])
        send_ref[:, cols] = jnp.where(first, m[64:], m[:64]).astype(BF16)


def join_kernel(*refs):
    *parts, out_ref = refs
    rows = parts[0].shape[0]
    for i, part in enumerate(parts):
        out_ref[i * rows : (i + 1) * rows] = part[...]


def fold_kernel(parts_ref, out_ref):
    total = parts_ref[0].astype(F32)
    for j in range(1, SPANS):
        total = total + parts_ref[j].astype(F32)
    total = total.astype(BF16)
    out_ref[:, 0, :] = total[:, :640]
    out_ref[:, 1, :512] = total[:, 640:]
    out_ref[:, 1, 512:] = jnp.zeros((ZS, 128), BF16)


def sum_kernel(parts_ref, out_ref):
    total = jnp.sum(parts_ref[...].astype(F32), axis=0)
    for j in range(9):
        row, col = j // 5, (j % 5) * 128
        out_ref[j] = total[row : row + 1, col : col + 128]


def columns(shift):
    pairs = []
    for z in range(ZS):
        for c in range(2):
            for s in range(SPANS):
                source = (z + c * 8 + s - 8 + shift) % ZS
                pairs.append(((source * 2 + c) * SPANS + s, (z * 2 + c) * SPANS + s))
    return pairs


def vmem(mib):
    return pltpu.CompilerParams(vmem_limit_bytes=mib << 20)


def local(queries, keys, values, proj_weight, gate_table, timestep, span_index, cotangent):
    S = jax.ShapeDtypeStruct
    swap = [(0, 1), (1, 0)]
    pair = pl.pallas_call(
        pair_kernel,
        out_shape=S((SPANS, 2 * TOK, HDM), BF16),
        in_specs=[pl.BlockSpec(memory_space=pltpu.HBM)] * 2,
        out_specs=pl.BlockSpec(memory_space=pl.ANY),
        scratch_shapes=[
            pltpu.VMEM((2, TOK, HDM), BF16),
            pltpu.SemaphoreType.DMA((2,)),
            pltpu.SemaphoreType.DMA((2 * SPANS,)),
        ],
        compiler_params=pltpu.CompilerParams(vmem_limit_bytes=67043328),
    )(keys, values)
    pairs = lax.all_to_all(pair, SEQ, 0, 0, tiled=True)
    every = ("z", "c") + SEQ
    mate = lax.ppermute(proj_weight[0], "c", swap)
    dozen = pl.pallas_call(
        pack_kernel,
        out_shape=S((16, CHUNK), BF16),
        in_specs=[VM, VM],
        out_specs=VM,
        compiler_params=vmem(8),
    )(proj_weight, mate)
    far = lax.ppermute(dozen, every, columns(16))
    near = lax.ppermute(dozen, every, columns(0))
    scaled, gate, bias = pl.pallas_call(
        scale_kernel,
        out_shape=(S((TOK, WIDTH), BF16), S((1, WIDTH), F32), S((1, SPANS * TOK), F32)),
        in_specs=[VM, VM, VM, VM],
        out_specs=(VM, VM, VM),
        compiler_params=vmem(8),
    )(timestep.reshape(1, 1), span_index.reshape(1, 1), cotangent, gate_table)
    keep, send, attended = pl.pallas_call(
        attend_kernel,
        out_shape=(S((SPANS, ZS, CHUNK), F32), S((SPANS, ZS, CHUNK), BF16), S((TOK, HDM), BF16)),
        in_specs=[VM, VM, VM, VM],
        out_specs=(VM, VM, VM),
        compiler_params=vmem(20),
    )(queries, pairs, scaled, bias)
    other = lax.ppermute(send, "c", swap)
    dozens = pl.pallas_call(
        join_kernel,
        out_shape=S((32, CHUNK), BF16),
        in_specs=[VM] * 2,
        out_specs=VM,
        compiler_params=vmem(8),
    )(near, far)
    beside = lax.ppermute(dozens, "yl", swap)
    block = pl.pallas_call(
        join_kernel,
        out_shape=S((64, CHUNK), BF16),
        in_specs=[VM] * 2,
        out_specs=VM,
        compiler_params=vmem(8),
    )(dozens, beside)
    both = pl.pallas_call(
        add_kernel,
        out_shape=S((SPANS, ZS, CHUNK), BF16),
        in_specs=[VM, VM],
        out_specs=VM,
        compiler_params=vmem(8),
    )(keep, other)
    parts = lax.all_to_all(both, SEQ, 0, 0, tiled=True)
    wide = pl.pallas_call(
        expand_kernel,
        out_shape=S((2, 4, TOK, 256), BF16),
        in_specs=[VM],
        out_specs=VM,
        compiler_params=vmem(8),
    )(attended)
    blocks = [block]
    for k in range(1, 4):
        blocks.append(lax.ppermute(block, "x", [(i, (i + k) % 4) for i in range(4)]))
    slices = pl.pallas_call(
        fold_kernel,
        out_shape=S((ZS, 2, 640), BF16),
        in_specs=[VM],
        out_specs=VM,
        compiler_params=vmem(8),
    )(parts)
    last = lax.all_to_all(slices, "z", 0, 0, tiled=True)
    weight_grad = pl.pallas_call(
        sum_kernel,
        out_shape=S((9, 1, 128), F32),
        in_specs=[VM],
        out_specs=VM,
        compiler_params=vmem(8),
    )(last).reshape(1, 9, 128)
    here = pl.pallas_call(
        join_kernel,
        out_shape=S((256, CHUNK), BF16),
        in_specs=[VM] * 4,
        out_specs=VM,
        compiler_params=vmem(8),
    )(*blocks)
    there = lax.ppermute(here, "c", swap)
    own, away = pl.pallas_call(
        mix_kernel,
        out_shape=(S((64, WIDTH), F32), S((64, WIDTH), BF16)),
        in_specs=[VM, VM, VM],
        out_specs=(VM, VM),
        compiler_params=vmem(12),
    )(wide, here, there)
    rest = lax.ppermute(away, "yh", swap)
    output = (gate * (own + rest.astype(F32))).astype(BF16)[None]
    return output, weight_grad


def solution(mesh):
    grid = Mesh(mesh.devices.reshape(ZS, 2, 2, 4, 2), ("z", "c", "yl", "x", "yh"))
    dp = ("z", "c")
    return jax.shard_map(
        local,
        mesh=grid,
        in_specs=(
            P(dp, SEQ, "yh"),
            P(dp, SEQ, "yh"),
            P(dp, SEQ, "yh"),
            P("yh", dp, None),
            P(),
            P(dp),
            P(dp),
            P(dp, SEQ, None),
        ),
        out_specs=(P(dp, SEQ + ("yh",), None), P("yh", dp + SEQ, None)),
        check_vma=False,
    )
```
